1024 devices in a mesh: context: 16 (over z), head: 64 (over y, x, core).
Axes of the slice: x: 4, y: 8, z: 16, core: 2. Of those that a mesh axis runs over, the one named last changes fastest.
Arguments:
- x_in: bfloat16 [16384, 16384], P('context', 'head'), may hold values from -6 to 6
- bc_in: bfloat16 [16384, 4096], P('context'), may hold values from -6 to 6
- z_in: bfloat16 [16384, 16384], P('context', 'head'), may hold values from -6 to 6
- dt_in: bfloat16 [256, 16384], P('head', 'context'), may hold values from -4 to 4
- conv_x_w: float32 [4, 16384], P(None, 'head'), may hold values from -3 to 3
- conv_x_b: float32 [16384], P('head'), may hold values from -1.5 to 1.5
- conv_bc_w: float32 [4, 4096], replicated, may hold values from -3 to 3
- conv_bc_b: float32 [4096], replicated, may hold values from -1.5 to 1.5
- dt_bias: float32 [256], P('head'), may hold values from -3.5 to -2.5
- a_log: float32 [256], P('head'), may hold values from -12 to 0
- skip_gain: float32 [256], P('head'), may hold values from 1 to 4
- norm_w: float32 [16384], P('head'), may hold values from 0.5 to 1.5
- doc_len: int32 [64], replicated, may hold values from 1 to 8192, 16384 in all
Outputs:
- ssd_out: bfloat16 [16384, 16384], P('context', 'head')
The draws below stay inside these ranges and needn't reach their ends.
Inputs may be any that keep to these rules, and one draw needn't show every extreme that they name: `doc_len`: the lengths sum to 16384; the longest is exactly 8192.
All inputs are finite; a program needn't handle non-finite values.
Results may differ from the reference program's by a relative error of at most 0.0034.
Values may be sent and summed in bfloat16 or wider, within the bound.
No kernel may reach another device: no remote copies, remote signals or barrier semaphores. Data moves between devices by JAX's collectives and lax.ppermute only.
A program may use at most 64 MiB of HBM per device.

```python
import math
import jax
import jax.numpy as jnp
import numpy as np
from jax import lax

HEAD_DIM = 64
STATE = 256
GROUPS = 8
CONV = 4
BLOCK = 256
HEADS = 256
TOKENS = 16384
DOCS = 64


def draw_a_log(key, part):
    pick_key, fast_key, slow_key = jax.random.split(key, 3)
    slow_share = 0.5
    slow_head = jax.random.bernoulli(pick_key, slow_share, (HEADS,))
    fast_log = jax.random.uniform(fast_key, (HEADS,), jnp.float32, jnp.log(0.3), 0.0)
    slow_log = jnp.log(40.0 / TOKENS) + jax.random.uniform(slow_key, (HEADS,), jnp.float32, jnp.log(0.05), jnp.log(2.0))
    return jnp.where(slow_head, slow_log, fast_log).astype(jnp.float32)


def level_of(rng, extent, pieces, smallest, high):
    gain = 1.0
    for position, blocks in pieces:
        steps = jax.random.uniform(jax.random.fold_in(jax.random.fold_in(rng, 6), position), (blocks,), jnp.float32, smallest / len(pieces), high / len(pieces))
        gain = gain * jnp.repeat(jnp.exp(steps), extent[position] // blocks).reshape((-1,) + (1,) * (len(extent) - 1 - position))
    return gain


def profile(number_of, total, reach, skew):
    loads = [(1 << 20) // math.isqrt(rank ** skew) + 1 for rank in range(2, number_of + 1)]
    spare, holding = total - reach - (number_of - 1), [1] * (number_of - 1)
    while spare > 0:
        movable = [i for i in range(number_of - 1) if holding[i] < reach]
        mass, left = sum([loads[i] for i in movable]), spare
        for i in movable:
            more = min(reach - holding[i], max(1, left * loads[i] // mass), spare)
            holding[i] = holding[i] + more
            spare = spare - more
    return np.array([reach] + holding)


def ragged_sizes(rng, number_of, total, bound, skew):
    if number_of == 2:
        one = jax.random.randint(rng, (), max(1, total - bound), min(bound, total - 1) + 1)
        return jnp.stack([one, total - one])
    tallies = jnp.asarray(profile(number_of, total, bound, skew), jnp.int32)
    twos = (number_of - 1) // 2
    source_of, receiver = tallies[1:1 + 2 * twos:2], tallies[2:2 + 2 * twos:2]
    room = jnp.minimum(source_of - 1, bound - receiver)
    shifted = jax.random.randint(jax.random.fold_in(rng, 1), (twos,), 0, 1 << 20) % (room + 1)
    tallies = tallies.at[1:1 + 2 * twos:2].set(source_of - shifted).at[2:2 + 2 * twos:2].set(receiver + shifted)
    return tallies[jax.random.permutation(jax.random.fold_in(rng, 2), number_of)]


def gaussian(own_key, dims, width, bound, pieces=(), kind=jnp.bfloat16):
    array = width * jax.random.normal(own_key, dims, jnp.float32)
    if pieces:
        array = array * level_of(own_key, dims, pieces, -0.22, 0.18)
    return jnp.clip(array, -bound, bound).astype(kind)


def setup_inputs(seed: int = 0) -> dict:
    seeds = jax.random.split(jax.random.key(seed), 14)
    x_in = gaussian(seeds[0], (TOKENS, HEADS * HEAD_DIM), 1.0, 6.0, ((0, 16), (1, 64)))
    bc_in = gaussian(seeds[1], (TOKENS, 2 * GROUPS * STATE), 1.0, 6.0, ((0, 16),))
    z_in = gaussian(seeds[2], (TOKENS, HEADS * HEAD_DIM), 1.0, 6.0, ((0, 16), (1, 64)))
    dt_in = gaussian(seeds[3], (HEADS, TOKENS), 1.0, 4.0, ((0, 64), (1, 16)))
    conv_x_w = gaussian(seeds[4], (CONV, HEADS * HEAD_DIM), CONV ** -0.5, 3.0, ((1, 64),), jnp.float32)
    conv_x_b = gaussian(seeds[5], (HEADS * HEAD_DIM,), 0.3, 1.5, ((0, 64),), jnp.float32)
    conv_bc_w = gaussian(seeds[6], (CONV, 2 * GROUPS * STATE), CONV ** -0.5, 3.0, (), jnp.float32)
    conv_bc_b = gaussian(seeds[7], (2 * GROUPS * STATE,), 0.3, 1.5, (), jnp.float32)
    dt_bias = jnp.clip(-3.5 + 1.0 * jax.random.uniform(seeds[8], (HEADS,), jnp.float32) ** level_of(seeds[8], (HEADS,), ((0, 64),), -0.2, 0.2), -3.5, -2.5)
    a_log = draw_a_log(jax.random.fold_in(seeds[13], 71), 0)
    skip_gain = jnp.clip(1.0 + 3.0 * jax.random.uniform(seeds[10], (HEADS,), jnp.float32) ** level_of(seeds[10], (HEADS,), ((0, 64),), -0.2, 0.2), 1.0, 4.0)
    norm_w = jnp.clip(1.0 + 0.1 * jax.random.normal(seeds[11], (HEADS * HEAD_DIM,), jnp.float32), 0.5, 1.5)
    doc_len = ragged_sizes(seeds[12], DOCS, TOKENS, TOKENS // 2, 2).astype(jnp.int32)
    return dict(x_in=x_in, bc_in=bc_in, z_in=z_in, dt_in=dt_in, conv_x_w=conv_x_w, conv_x_b=conv_x_b, conv_bc_w=conv_bc_w, conv_bc_b=conv_bc_b, dt_bias=dt_bias, a_log=a_log, skip_gain=skip_gain, norm_w=norm_w, doc_len=doc_len)


exact_mode = lax.Precision.HIGHEST
norm_floor = 1e-05

def doc_marks(doc_len, positions):
    doc_ends = jnp.cumsum(doc_len).astype(jnp.int32)
    begins = doc_ends - doc_len
    segment = lax.optimization_barrier(jnp.sum((doc_ends[None, :] <= positions[:, None]).astype(jnp.int32), axis=1))
    opening = lax.optimization_barrier(jnp.sum((begins[None, :] == positions[:, None]).astype(jnp.int32), axis=1))
    return (segment, opening)

def conv_silu(extended, segment_ext, weights, biases, rows_count):
    newest = segment_ext[CONV - 1:CONV - 1 + rows_count]
    summed = jnp.zeros((rows_count, extended.shape[1]), jnp.float32) + biases[None, :]
    for offset in range(CONV):
        same_doc = (segment_ext[offset:offset + rows_count] == newest).astype(jnp.float32)
        summed = summed + weights[offset][None, :] * extended[offset:offset + rows_count].astype(jnp.float32) * same_doc[:, None]
    return jax.nn.silu(summed).astype(jnp.bfloat16)

def reference(x_in, bc_in, z_in, dt_in, conv_x_w, conv_x_b, conv_bc_w, conv_bc_b, dt_bias, a_log, skip_gain, norm_w, doc_len):
    rows_all = x_in.shape[0]
    per_group = HEADS // GROUPS
    group_width = per_group * HEAD_DIM
    positions = jnp.arange(rows_all, dtype=jnp.int32)
    segment, opening = doc_marks(doc_len, positions)
    segment_ext = jnp.concatenate([jnp.zeros((CONV - 1,), jnp.int32), segment])
    blocks = rows_all // BLOCK
    seg_blocks = segment.reshape(blocks, BLOCK)
    alive_mask = jnp.cumsum(opening.reshape(blocks, BLOCK), axis=1) == 0
    lower_tri = jnp.arange(BLOCK)[:, None] >= jnp.arange(BLOCK)[None, :]
    same_block = (seg_blocks[:, :, None] == seg_blocks[:, None, :]) & lower_tri[None]
    tail_same = seg_blocks == seg_blocks[:, -1:]

    def one_group(group_index):
        x_part = lax.dynamic_slice_in_dim(x_in, group_index * group_width, group_width, 1)
        b_part = lax.dynamic_slice_in_dim(bc_in, group_index * STATE, STATE, 1)
        c_part = lax.dynamic_slice_in_dim(bc_in, (GROUPS + group_index) * STATE, STATE, 1)
        raw_rows = jnp.concatenate([x_part, b_part, c_part], axis=1)
        extended = jnp.concatenate([jnp.zeros((CONV - 1, raw_rows.shape[1]), jnp.bfloat16), raw_rows], axis=0)
        weights = jnp.concatenate([lax.dynamic_slice_in_dim(conv_x_w, group_index * group_width, group_width, 1), lax.dynamic_slice_in_dim(conv_bc_w, group_index * STATE, STATE, 1), lax.dynamic_slice_in_dim(conv_bc_w, (GROUPS + group_index) * STATE, STATE, 1)], axis=1)
        biases = jnp.concatenate([lax.dynamic_slice_in_dim(conv_x_b, group_index * group_width, group_width, 0), lax.dynamic_slice_in_dim(conv_bc_b, group_index * STATE, STATE, 0), lax.dynamic_slice_in_dim(conv_bc_b, (GROUPS + group_index) * STATE, STATE, 0)], axis=0)
        mixed = conv_silu(extended, segment_ext, weights, biases, rows_all)
        b_vals = mixed[:, group_width:group_width + STATE].astype(jnp.float32).reshape(blocks, BLOCK, STATE)
        c_vals = mixed[:, group_width + STATE:].astype(jnp.float32).reshape(blocks, BLOCK, STATE)
        inner_prod = jnp.einsum('ctn,csn->cts', c_vals, b_vals, precision=exact_mode)

        def one_head(local_head):
            head_global = group_index * per_group + local_head
            x_head = lax.dynamic_slice_in_dim(mixed, local_head * HEAD_DIM, HEAD_DIM, 1).astype(jnp.float32)
            dt_row = lax.dynamic_index_in_dim(dt_in, head_global, 0, keepdims=False).astype(jnp.float32)
            step_size = jax.nn.softplus(dt_row + dt_bias[head_global])
            rate_value = -jnp.exp(a_log[head_global])
            weighted = (x_head * step_size[:, None]).reshape(blocks, BLOCK, HEAD_DIM)
            running = jnp.cumsum((step_size * rate_value).reshape(blocks, BLOCK), axis=1)
            gap_logs = jnp.minimum(running[:, :, None] - running[:, None, :], 0.0)
            mixing = jnp.where(same_block, jnp.exp(gap_logs), 0.0) * inner_prod
            intra_out = jnp.einsum('cts,csp->ctp', mixing, weighted, precision=exact_mode)
            tail_weight = jnp.where(tail_same, jnp.exp(running[:, -1:] - running), 0.0)
            summaries = jnp.einsum('csp,csn->cpn', weighted * tail_weight[:, :, None], b_vals, precision=exact_mode)
            carry_decay = jnp.exp(running[:, -1]) * alive_mask[:, -1].astype(jnp.float32)

            def advance(state_now, inputs):
                summary, factor = inputs
                return (factor * state_now + summary, state_now)
            _, incoming = lax.scan(advance, jnp.zeros((HEAD_DIM, STATE), jnp.float32), (summaries, carry_decay))
            entry_scale = alive_mask.astype(jnp.float32) * jnp.exp(running)
            from_state = jnp.einsum('ctn,cpn->ctp', c_vals, incoming, precision=exact_mode) * entry_scale[:, :, None]
            return (intra_out + from_state).reshape(rows_all, HEAD_DIM) + skip_gain[head_global] * x_head
        per_head = lax.map(one_head, jnp.arange(per_group, dtype=jnp.int32))
        outputs = jnp.transpose(per_head, (1, 0, 2)).reshape(rows_all, group_width)
        z_part = lax.dynamic_slice_in_dim(z_in, group_index * group_width, group_width, 1).astype(jnp.float32)
        return outputs * jax.nn.silu(z_part)
    group_outs = lax.map(one_group, jnp.arange(GROUPS, dtype=jnp.int32))
    square_sum = lax.optimization_barrier(jnp.sum(lax.optimization_barrier(jnp.sum(group_outs * group_outs, axis=2)), axis=0))
    scale_rows = lax.rsqrt(square_sum / (HEADS * HEAD_DIM) + norm_floor)
    gated_all = jnp.transpose(group_outs, (1, 0, 2)).reshape(rows_all, HEADS * HEAD_DIM)
    return (gated_all * scale_rows[:, None] * norm_w[None, :]).astype(jnp.bfloat16)
```

```python
import jax
import jax.numpy as jnp
from jax import lax
from jax.sharding import PartitionSpec as P

HEAD_DIM = 64
STATE = 256
GROUPS = 8
CONV = 4
BLOCK = 256


norm_floor = 1e-05


def from_behind(shard, axis, by):
    count = lax.axis_size(axis)
    pairs = [(i, i + by) for i in range(count) if 0 <= i + by < count]
    return lax.ppermute(shard, axis, pairs)


def split_pair(value):
    high = value.astype(jnp.bfloat16)
    return high, (value - high.astype(jnp.float32)).astype(jnp.bfloat16)


def entering_state(decay, end):
    count = lax.axis_size("context")
    heads, dim, state = end.shape
    width = heads * dim // count
    slices = end.astype(jnp.bfloat16).reshape(count, width // 2, 2 * state)
    high, rest = split_pair(decay)
    middle, low = split_pair(decay - high.astype(jnp.float32))
    parts = jnp.repeat(jnp.stack([high, middle, low], axis=1), count // heads, axis=0)
    parts = jnp.pad(parts, ((0, 0), (0, 125)))
    extra = jnp.broadcast_to(parts[:, None, :], (count, width // 2, 128))
    sent = jnp.concatenate([slices, extra], axis=2)
    got = lax.all_to_all(sent, "context", split_axis=0, concat_axis=0, tiled=True)
    got = got.astype(jnp.float32)
    factors = jnp.sum(got[:, 0, 2 * state : 2 * state + 3], axis=1)
    ends = got[:, :, : 2 * state]
    now = jnp.zeros_like(ends[0])
    entering = []
    for shard in range(count):
        entering.append(now)
        now = factors[shard] * now + ends[shard]
    back = jnp.stack(entering).astype(jnp.bfloat16)
    mine = lax.all_to_all(back, "context", split_axis=0, concat_axis=0, tiled=True)
    return mine.reshape(heads, dim, state)


def taken_together(shard, axis):
    count = lax.axis_size(axis)
    tile = shard.astype(jnp.bfloat16).reshape(1, -1, 128)
    copies = jnp.broadcast_to(tile, (count, *tile.shape[1:]))
    everything = lax.all_to_all(copies, axis, split_axis=0, concat_axis=0, tiled=True)
    return jnp.sum(everything.astype(jnp.float32), axis=0).reshape(shard.shape)


def doc_marks(doc_len, positions):
    doc_ends = jnp.cumsum(doc_len)
    begins = doc_ends - doc_len
    segment = jnp.sum((doc_ends[None, :] <= positions[:, None]).astype(jnp.int32), axis=1)
    opening = jnp.sum((begins[None, :] == positions[:, None]).astype(jnp.int32), axis=1)
    return (segment, opening)


def conv_silu(extended, segment_ext, weights, biases, rows_count):
    newest = segment_ext[CONV - 1 : CONV - 1 + rows_count]
    summed = jnp.zeros((rows_count, extended.shape[1]), jnp.float32) + biases[None, :]
    for offset in range(CONV):
        same_doc = (segment_ext[offset : offset + rows_count] == newest).astype(jnp.float32)
        summed = (
            summed
            + weights[offset][None, :]
            * extended[offset : offset + rows_count].astype(jnp.float32)
            * same_doc[:, None]
        )
    return jax.nn.silu(summed).astype(jnp.bfloat16)


def product(spec, left, right):
    return jnp.einsum(spec, left, right, preferred_element_type=jnp.float32)


def shards(
    x_in,
    bc_in,
    z_in,
    dt_in,
    conv_x_w,
    conv_x_b,
    conv_bc_w,
    conv_bc_b,
    dt_bias,
    a_log,
    skip_gain,
    norm_w,
    doc_len,
):
    rows_here = x_in.shape[0]
    heads_here = dt_in.shape[0]
    width_here = x_in.shape[1]
    heads_total = heads_here * lax.axis_size("head")
    per_group = heads_total // GROUPS
    group_index = lax.axis_index("head") * heads_here // per_group
    b_raw = lax.dynamic_slice_in_dim(bc_in, group_index * STATE, STATE, 1)
    c_raw = lax.dynamic_slice_in_dim(bc_in, (GROUPS + group_index) * STATE, STATE, 1)
    raw_rows = jnp.concatenate([x_in, b_raw, c_raw], axis=1)
    weights = jnp.concatenate(
        [
            conv_x_w,
            lax.dynamic_slice_in_dim(conv_bc_w, group_index * STATE, STATE, 1),
            lax.dynamic_slice_in_dim(conv_bc_w, (GROUPS + group_index) * STATE, STATE, 1),
        ],
        axis=1,
    )
    biases = jnp.concatenate(
        [
            conv_x_b,
            lax.dynamic_slice_in_dim(conv_bc_b, group_index * STATE, STATE, 0),
            lax.dynamic_slice_in_dim(conv_bc_b, (GROUPS + group_index) * STATE, STATE, 0),
        ],
        axis=0,
    )
    before = from_behind(raw_rows[rows_here - (CONV - 1) :], "context", 1)
    extended = jnp.concatenate([before, raw_rows], axis=0)
    first_pos = lax.axis_index("context") * rows_here
    positions_ext = first_pos - (CONV - 1) + jnp.arange(rows_here + CONV - 1, dtype=jnp.int32)
    segment_ext, opening_ext = doc_marks(doc_len, positions_ext)
    mixed = conv_silu(extended, segment_ext, weights, biases, rows_here)
    segment = segment_ext[CONV - 1 :]
    opening = opening_ext[CONV - 1 :]
    blocks = rows_here // BLOCK
    x_vals = mixed[:, :width_here].astype(jnp.float32).reshape(blocks, BLOCK, heads_here, HEAD_DIM)
    b_vals = mixed[:, width_here : width_here + STATE].reshape(blocks, BLOCK, STATE)
    c_vals = mixed[:, width_here + STATE :].reshape(blocks, BLOCK, STATE)
    step_size = jax.nn.softplus(dt_in.astype(jnp.float32) + dt_bias[:, None])
    log_decay = (step_size * (-jnp.exp(a_log))[:, None]).reshape(heads_here, blocks, BLOCK)
    running = jnp.cumsum(log_decay, axis=2)
    step_blocks = jnp.transpose(step_size.reshape(heads_here, blocks, BLOCK), (1, 2, 0))
    weighted = x_vals * step_blocks[..., None]
    seg_blocks = segment.reshape(blocks, BLOCK)
    alive_mask = jnp.cumsum(opening.reshape(blocks, BLOCK), axis=1) == 0
    lower_tri = jnp.arange(BLOCK)[:, None] >= jnp.arange(BLOCK)[None, :]
    same_block = (seg_blocks[:, :, None] == seg_blocks[:, None, :]) & lower_tri[None]
    inner_prod = product("ctn,csn->cts", c_vals, b_vals)
    gap_logs = jnp.minimum(running[:, :, :, None] - running[:, :, None, :], 0.0)
    mixing = jnp.where(same_block[None], jnp.exp(gap_logs), 0.0) * inner_prod[None]
    step_here = step_size.reshape(heads_here, blocks, 1, BLOCK)
    mixing = (mixing * step_here).astype(jnp.bfloat16)
    x_low = mixed[:, :width_here].reshape(blocks, BLOCK, heads_here, HEAD_DIM)
    intra_out = product("hcts,cshp->cthp", mixing, x_low)
    tail_weight = jnp.where(
        (seg_blocks == seg_blocks[:, -1:])[None], jnp.exp(running[:, :, -1:] - running), 0.0
    )
    tail_blocks = jnp.transpose(tail_weight, (1, 2, 0))
    high, low = split_pair(weighted * tail_blocks[..., None])
    summaries = product("cshp,csn->chpn", high, b_vals) + product("cshp,csn->chpn", low, b_vals)
    carry_decay = jnp.transpose(
        jnp.exp(running[:, :, -1]) * alive_mask[None, :, -1].astype(jnp.float32)
    )

    state_now = jnp.zeros((heads_here, HEAD_DIM, STATE), jnp.float32)
    decay_now = jnp.ones((heads_here,), jnp.float32)
    local_in, decay_in = [], []
    for block in range(blocks):
        local_in.append(state_now)
        decay_in.append(decay_now)
        state_now = carry_decay[block][:, None, None] * state_now + summaries[block]
        decay_now = decay_now * carry_decay[block]
    local_in = jnp.stack(local_in).astype(jnp.bfloat16)
    decay_in = jnp.stack(decay_in)
    entering = entering_state(decay_now, state_now)
    entry_scale = jnp.transpose(alive_mask[None].astype(jnp.float32) * jnp.exp(running), (1, 2, 0))
    from_state = product("ctn,chpn->cthp", c_vals, local_in)
    from_before = product("ctn,hpn->cthp", c_vals, entering) * decay_in[:, None, :, None]
    from_state = (from_state + from_before) * entry_scale[..., None]
    outputs = intra_out + from_state + skip_gain[None, None, :, None] * x_vals
    outputs = outputs.reshape(rows_here, width_here)
    gated_out = outputs * jax.nn.silu(z_in.astype(jnp.float32))
    squares = jnp.sum(gated_out * gated_out, axis=1)
    total_squares = taken_together(squares, "head")
    mean_square = total_squares / (heads_total * HEAD_DIM)
    result = gated_out * lax.rsqrt(mean_square + norm_floor)[:, None] * norm_w[None, :]
    return result.astype(jnp.bfloat16)


def solution(mesh):
    return jax.shard_map(
        shards,
        mesh=mesh,
        in_specs=(
            P("context", "head"),
            P("context", None),
            P("context", "head"),
            P("head", "context"),
            P(None, "head"),
            P("head"),
            P(),
            P(),
            P("head"),
            P("head"),
            P("head"),
            P("head"),
            P(),
        ),
        out_specs=P("context", "head"),
        check_vma=False,
    )
```

```python
import functools

import jax
import jax.numpy as jnp
from jax import lax
from jax.experimental import pallas as pl
from jax.experimental.pallas import tpu as pltpu
from jax.sharding import PartitionSpec as P

HEAD_DIM = 64
STATE = 256
GROUPS = 8
CONV = 4
BLOCK = 256
HALO = 8

norm_floor = 1e-05
f32 = jnp.float32
bf16 = jnp.bfloat16
exact_mode = lax.Precision.HIGHEST


def dot(left, right, precision=None):
    return jnp.dot(left, right, preferred_element_type=f32, precision=precision)


def dot_rows(left, right, precision=None):
    return lax.dot_general(
        left, right, (((1,), (1,)), ((), ())), preferred_element_type=f32, precision=precision
    )


def iota(shape, axis):
    return lax.broadcasted_iota(jnp.int32, shape, axis)


def silu(value):
    half = 0.5 * value
    return half + half * jnp.tanh(half)


def split_pair(value):
    high = value.astype(bf16)
    return high, (value - high.astype(f32)).astype(bf16)


def doc_starts(doc_len, first):
    count = doc_len.shape[1]
    lengths = doc_len.astype(f32)
    row, column = iota((count, count), 0), iota((count, count), 1)
    down = jnp.sum(jnp.where(row == column, lengths, 0.0), axis=1, keepdims=True)
    begins = jnp.sum(jnp.where(row < column, down, 0.0), axis=0, keepdims=True)
    places = (iota((BLOCK, 1), 0) + first).astype(f32)
    starts = jnp.max(jnp.where(begins <= places, begins, -1.0), axis=1, keepdims=True)
    return starts, places


def steps(dt, dt_bias, a_log):
    heads = dt.shape[0]
    values = jnp.concatenate([dt.astype(f32)] * (8 // heads), axis=0)
    row = iota((8, 1), 0) % heads
    bias = jnp.zeros((8, 1), f32)
    log_rate = jnp.zeros((8, 1), f32)
    for head in range(heads):
        bias = jnp.where(row == head, dt_bias[head], bias)
        log_rate = jnp.where(row == head, a_log[head], log_rate)
    values = values + bias
    step = jnp.maximum(values, 0.0) + jnp.log1p(jnp.exp(-jnp.abs(values)))
    return step, step * -jnp.exp(log_rate)


def conv_silu(block, ext, before, raw, weights, bias, age):
    @pl.when(block == 0)
    def _():
        ext[0:HALO] = before.astype(f32)

    @pl.when(block > 0)
    def _():
        ext[0:HALO] = ext[BLOCK : BLOCK + HALO]

    now = raw.astype(f32)
    ext[HALO : HALO + BLOCK] = now
    summed = bias + weights[CONV - 1 : CONV] * now
    for back in range(1, CONV):
        kept = jnp.where(age >= back, 1.0, 0.0)
        older = ext[HALO - back : HALO - back + BLOCK]
        summed = summed + weights[CONV - 1 - back : CONV - back] * (older * kept)
    return silu(summed).astype(bf16)


def wide_row(ref, at):
    return jnp.concatenate([ref[pl.ds(at, 1), :], ref[pl.ds(at + 1, 1), :]], axis=1)


def ends_kernel(
    place, x_in, b_in, halo, dt_in, x_w, x_b, b_w, b_b, dt_bias, a_log, doc_len,
    x_out, b_out, states_out, sent, ext_x, ext_b, state, total,
):
    block = pl.program_id(0)
    blocks = pl.num_programs(0)
    group, first = place[0], place[1]
    start, places = doc_starts(doc_len[...], first + block * BLOCK)
    age = places - start
    width = x_in.shape[1]
    x = conv_silu(block, ext_x, halo[:, :width], x_in[...], x_w[...], wide_row(x_b, 0), age)
    b = conv_silu(
        block, ext_b, halo[:, width : width + STATE], b_in[...], b_w[...],
        wide_row(b_b, 2 * group), age,
    )
    x_out[...] = x
    b_out[...] = b
    step, decay = steps(dt_in[...], dt_bias, a_log)
    upto = (iota((BLOCK, BLOCK), 0) <= iota((BLOCK, BLOCK), 1)).astype(f32)
    running = dot(decay, upto, exact_mode)
    last = running[:, BLOCK - 1 : BLOCK]
    last_start = start[BLOCK - 1 : BLOCK]
    ahead = (iota((1, BLOCK), 1) + first + block * BLOCK).astype(f32)
    tail = jnp.where(ahead >= last_start, jnp.exp(last - running), 0.0) * step
    block_start = (first + block * BLOCK).astype(f32)
    carry = jnp.where(last_start < block_start, jnp.exp(last), 0.0)

    @pl.when(block == 0)
    def _():
        state[...] = jnp.zeros_like(state)
        total[...] = jnp.zeros_like(total)

    heads = dt_in.shape[0]
    old = state[...]
    states_out[0] = old.astype(bf16)
    across = jnp.transpose(x.astype(f32))
    scaled, kept = [], []
    for head in range(heads):
        rows = slice(head * HEAD_DIM, (head + 1) * HEAD_DIM)
        scaled.append(across[rows] * tail[head : head + 1])
        kept.append(old[rows] * carry[head : head + 1])
    high, low = split_pair(jnp.concatenate(scaled, axis=0))
    new = jnp.concatenate(kept, axis=0) + dot(high, b) + dot(low, b)
    state[...] = new
    total[...] = total[...] + last

    @pl.when(block == blocks - 1)
    def _():
        count = sent.shape[0]
        shard_start = first.astype(f32)
        through = jnp.where(last_start < shard_start, jnp.exp(total[...]), 0.0)
        top = through.astype(bf16).astype(f32)
        middle = (through - top).astype(bf16).astype(f32)
        rest = through - top - middle
        lane = iota((8, 128), 1)
        for piece in range(count):
            rows = 2 * HALO * piece
            head = piece * heads // count
            sent[piece, :, :STATE] = new[rows : rows + HALO].astype(bf16)
            sent[piece, :, STATE : 2 * STATE] = new[rows + HALO : rows + 2 * HALO].astype(bf16)
            one = slice(head, head + 1)
            extra = jnp.where(lane == 0, top[one], jnp.where(lane == 1, middle[one], rest[one]))
            sent[piece, :, 2 * STATE :] = extra.astype(bf16)


def spread(columns):
    lane = iota((BLOCK, 128), 1)
    return jnp.concatenate(
        [
            jnp.where(lane < HEAD_DIM, columns[:, at : at + 1], columns[:, at + 1 : at + 2])
            for at in (0, 2)
        ],
        axis=1,
    )


def inside_kernel(
    place, x_ref, b_ref, c_in, z_in, halo, dt_in, c_w, c_b, states, dt_bias, a_log, skip, doc_len,
    c_out, base_out, gain_out, ext_c, total,
):
    block = pl.program_id(0)
    group, first = place[0], place[1]
    start, places = doc_starts(doc_len[...], first + block * BLOCK)
    c = conv_silu(
        block, ext_c, halo[:, 2 * STATE : 3 * STATE], c_in[...], c_w[...],
        wide_row(c_b, 2 * (GROUPS + group)), places - start,
    )
    c_out[...] = c
    step, decay = steps(dt_in[...], dt_bias, a_log)
    older = iota((BLOCK, BLOCK), 1) <= iota((BLOCK, BLOCK), 0)
    tri = older.astype(f32)
    down = dot_rows(tri, decay, exact_mode)
    running = dot_rows(decay, tri, exact_mode)
    ahead = (iota((1, BLOCK), 1) + first + block * BLOCK).astype(f32)
    same = older & (ahead >= start)
    inner = dot_rows(c, b_ref[...])
    x = x_ref[...]
    x_wide = x.astype(f32)
    column = iota((BLOCK, x.shape[1]), 1)
    heads = dt_in.shape[0]
    y = jnp.zeros((BLOCK, x.shape[1]), f32)
    gains = jnp.zeros((1, x.shape[1]), f32)
    for head in range(heads):
        gap = jnp.minimum(down[:, head : head + 1] - running[head : head + 1], 0.0)
        mixing = jnp.where(same, jnp.exp(gap), 0.0) * step[head : head + 1] * inner
        own = (column >= head * HEAD_DIM) & (column < (head + 1) * HEAD_DIM)
        y = y + dot(mixing.astype(bf16), jnp.where(own, x_wide, 0.0).astype(bf16))
        gains = jnp.where(own[0:1], skip[head], gains)

    @pl.when(block == 0)
    def _():
        total[...] = jnp.zeros_like(total)

    block_start = (first + block * BLOCK).astype(f32)
    local = jnp.where(start < block_start, jnp.exp(down), 0.0)
    far = jnp.where(start < first.astype(f32), jnp.exp(down + total[...]), 0.0)
    total[...] = total[...] + down[BLOCK - 1 : BLOCK]
    y = y + dot_rows(c, states[0]) * spread(local) + gains * x_wide
    gate = silu(z_in[...].astype(f32))
    base_out[...] = y * gate
    gain_out[...] = spread(far) * gate


def scan_kernel(got, back):
    now = jnp.zeros((HALO, 2 * STATE), f32)
    for shard in range(got.shape[0]):
        back[shard] = now.astype(bf16)
        message = got[shard].astype(f32)
        at = 2 * STATE
        factor = message[0:1, at : at + 1] + message[0:1, at + 1 : at + 2]
        factor = factor + message[0:1, at + 2 : at + 3]
        now = factor * now + message[:, :at]


def join_kernel(mine, c_ref, base, gain, gated_out, copies, entering, squares):
    block = pl.program_id(0)

    @pl.when(block == 0)
    def _():
        rows = []
        for piece in range(mine.shape[0]):
            part = mine[piece].astype(f32)
            rows += [part[:, :STATE], part[:, STATE:]]
        entering[...] = jnp.concatenate(rows, axis=0).astype(bf16)

    gated = base[...] + gain[...] * dot_rows(c_ref[...], entering[...])
    gated_out[...] = gated
    high, low = split_pair(gated * gated)
    ones = jnp.ones((8, gated.shape[1]), bf16)
    sums = dot_rows(ones, high) + dot_rows(ones, low)
    squares[pl.ds(2 * block, 1), :] = sums[0:1, :128]
    squares[pl.ds(2 * block + 1, 1), :] = sums[0:1, 128:]

    @pl.when(block == pl.num_programs(0) - 1)
    def _():
        copies[...] = jnp.broadcast_to(squares[...].astype(bf16)[None], copies.shape)


def finish_kernel(channels, everything, gated, norm, out, scale):
    block = pl.program_id(0)

    @pl.when(block == 0)
    def _():
        total = jnp.sum(everything[...].astype(f32), axis=0)
        scale[...] = lax.rsqrt(total / channels + norm_floor)

    same = iota((128, 128), 0) == iota((128, 128), 1)
    columns = []
    for half in range(2):
        row = scale[pl.ds(2 * block + half, 1), :]
        columns.append(jnp.sum(jnp.where(same, row, 0.0), axis=1, keepdims=True))
    column = jnp.concatenate(columns, axis=0)
    out[...] = (gated[...] * column * wide_row(norm, 0)).astype(bf16)


def shards(
    x_in, bc_in, z_in, dt_in, conv_x_w, conv_x_b, conv_bc_w, conv_bc_b, dt_bias, a_log,
    skip_gain, norm_w, doc_len,
):
    rows, width = x_in.shape
    heads = dt_in.shape[0]
    heads_total = heads * lax.axis_size("head")
    per_group = heads_total // GROUPS
    group = lax.axis_index("head") * heads // per_group
    place = jnp.stack([group, lax.axis_index("context") * rows]).astype(jnp.int32)
    shard_count = lax.axis_size("context")
    head_count = lax.axis_size("head")
    blocks = rows // BLOCK

    bc_last = bc_in[rows - HALO :]
    last = jnp.concatenate(
        [
            x_in[rows - HALO :],
            lax.dynamic_slice_in_dim(bc_last, group * STATE, STATE, 1),
            lax.dynamic_slice_in_dim(bc_last, (GROUPS + group) * STATE, STATE, 1),
        ],
        axis=1,
    )
    pairs = [(i, i + 1) for i in range(shard_count - 1)]
    halo = lax.ppermute(last, "context", pairs)
    x_b = conv_x_b.reshape(-1, 128)
    bc_b = conv_bc_b.reshape(-1, 128)
    norm = norm_w.reshape(-1, 128)
    docs = doc_len.reshape(1, -1)

    def whole(*shape):
        return pl.BlockSpec(shape, lambda i, *_: (0,) * len(shape))

    tokens = pl.BlockSpec((BLOCK, width), lambda i, *_: (i, 0))
    b_cols = pl.BlockSpec((BLOCK, STATE), lambda i, s: (i, s[0]))
    c_cols = pl.BlockSpec((BLOCK, STATE), lambda i, s: (i, s[0] + GROUPS))
    b_taps = pl.BlockSpec((CONV, STATE), lambda i, s: (0, s[0]))
    c_taps = pl.BlockSpec((CONV, STATE), lambda i, s: (0, s[0] + GROUPS))
    dt_cols = pl.BlockSpec((heads, BLOCK), lambda i, *_: (0, i))
    scalars = pl.BlockSpec(memory_space=pltpu.SMEM)
    block_states = pl.BlockSpec((1, width, STATE), lambda i, *_: (i, 0, 0))

    def call(kernel, prefetch, in_specs, out_specs, out_shape, scratch, grid=(blocks,), cost=5e8):
        return pl.pallas_call(
            kernel,
            grid_spec=pltpu.PrefetchScalarGridSpec(
                num_scalar_prefetch=prefetch,
                grid=grid,
                in_specs=in_specs,
                out_specs=out_specs,
                scratch_shapes=scratch,
            ),
            out_shape=out_shape,
            cost_estimate=pl.CostEstimate(
                flops=int(cost), bytes_accessed=4_000_000, transcendentals=1_000_000
            ),
        )

    struct = jax.ShapeDtypeStruct
    message = 2 * STATE + 128
    x, b, states, sent = call(
        ends_kernel,
        1,
        [
            tokens, b_cols, whole(HALO, width + 2 * STATE), dt_cols, whole(CONV, width),
            whole(*x_b.shape), b_taps, whole(*bc_b.shape), scalars, scalars, whole(*docs.shape),
        ],
        [tokens, tokens, block_states, whole(shard_count, HALO, message)],
        [
            struct((rows, width), bf16),
            struct((rows, STATE), bf16),
            struct((blocks, width, STATE), bf16),
            struct((shard_count, HALO, message), bf16),
        ],
        [
            pltpu.VMEM((BLOCK + HALO, width), f32),
            pltpu.VMEM((BLOCK + HALO, STATE), f32),
            pltpu.VMEM((width, STATE), f32),
            pltpu.VMEM((8, 1), f32),
        ],
    )(place, x_in, bc_in, halo, dt_in, conv_x_w, x_b, conv_bc_w, bc_b, dt_bias, a_log, docs)
    got = lax.all_to_all(sent, "context", split_axis=0, concat_axis=0, tiled=True)
    c, base, gain = call(
        inside_kernel,
        1,
        [
            tokens, tokens, c_cols, tokens, whole(HALO, width + 2 * STATE), dt_cols, c_taps,
            whole(*bc_b.shape), block_states, scalars, scalars, scalars, whole(*docs.shape),
        ],
        [tokens, tokens, tokens],
        [
            struct((rows, STATE), bf16),
            struct((rows, width), f32),
            struct((rows, width), f32),
        ],
        [pltpu.VMEM((BLOCK + HALO, STATE), f32), pltpu.VMEM((1, 8), f32)],
    )(
        place, x, b, bc_in, z_in, halo, dt_in, conv_bc_w, bc_b, states, dt_bias, a_log,
        skip_gain, docs,
    )
    back = pl.pallas_call(
        scan_kernel, out_shape=struct((shard_count, HALO, 2 * STATE), bf16)
    )(got)
    mine = lax.all_to_all(back, "context", split_axis=0, concat_axis=0, tiled=True)
    gated, copies = call(
        join_kernel,
        0,
        [whole(shard_count, HALO, 2 * STATE), tokens, tokens, tokens],
        [tokens, whole(head_count, rows // 128, 128)],
        [struct((rows, width), f32), struct((head_count, rows // 128, 128), bf16)],
        [pltpu.VMEM((width, STATE), bf16), pltpu.VMEM((rows // 128, 128), f32)],
    )(mine, c, base, gain)
    everything = lax.all_to_all(copies, "head", split_axis=0, concat_axis=0, tiled=True)
    return call(
        functools.partial(finish_kernel, float(heads_total * HEAD_DIM)),
        0,
        [whole(head_count, rows // 128, 128), tokens, whole(*norm.shape)],
        tokens,
        struct((rows, width), bf16),
        [pltpu.VMEM((rows // 128, 128), f32)],
    )(everything, gated, norm)


def solution(mesh):
    return jax.shard_map(
        shards,
        mesh=mesh,
        in_specs=(
            P("context", "head"),
            P("context", None),
            P("context", "head"),
            P("head", "context"),
            P(None, "head"),
            P("head"),
            P(),
            P(),
            P("head"),
            P("head"),
            P("head"),
            P("head"),
            P(),
        ),
        out_specs=P("context", "head"),
        check_vma=False,
    )
```

```python
import functools

import jax
import jax.numpy as jnp
from jax import lax
from jax.experimental import pallas as pl
from jax.experimental.pallas import tpu as pltpu
from jax.sharding import PartitionSpec as P

HEAD_DIM = 64
STATE = 256
GROUPS = 8
CONV = 4
BLOCK = 256
HALO = 8
GRANT = 16 * 1024 * 1024
WIDE_GRANT = 46 * 1024 * 1024

norm_floor = 1e-05
f32 = jnp.float32
bf16 = jnp.bfloat16
exact_mode = lax.Precision.HIGHEST


def dot(left, right, precision=None):
    return jnp.dot(left, right, preferred_element_type=f32, precision=precision)


def dot_rows(left, right, precision=None):
    return lax.dot_general(
        left, right, (((1,), (1,)), ((), ())), preferred_element_type=f32, precision=precision
    )


def iota(shape, axis):
    return lax.broadcasted_iota(jnp.int32, shape, axis)


def silu(value):
    half = 0.5 * value
    return half + half * jnp.tanh(half)


def split_pair(value):
    high = value.astype(bf16)
    return high, (value - high.astype(f32)).astype(bf16)


def doc_starts(doc_len, first):
    count = doc_len.shape[1]
    lengths = doc_len.astype(f32)
    row, column = iota((count, count), 0), iota((count, count), 1)
    down = jnp.sum(jnp.where(row == column, lengths, 0.0), axis=1, keepdims=True)
    begins = jnp.sum(jnp.where(row < column, down, 0.0), axis=0, keepdims=True)
    places = (iota((BLOCK, 1), 0) + first).astype(f32)
    starts = jnp.max(jnp.where(begins <= places, begins, -1.0), axis=1, keepdims=True)
    return starts, places


def steps(dt, dt_bias, a_log):
    heads = dt.shape[0]
    values = jnp.concatenate([dt.astype(f32)] * (8 // heads), axis=0)
    row = iota((8, 1), 0) % heads
    bias = jnp.zeros((8, 1), f32)
    log_rate = jnp.zeros((8, 1), f32)
    for head in range(heads):
        bias = jnp.where(row == head, dt_bias[head], bias)
        log_rate = jnp.where(row == head, a_log[head], log_rate)
    values = values + bias
    step = jnp.maximum(values, 0.0) + jnp.log1p(jnp.exp(-jnp.abs(values)))
    return step, step * -jnp.exp(log_rate)


def conv_silu(block, ext, before, raw, weights, bias, age):
    @pl.when(block == 0)
    def _():
        ext[0:HALO] = before.astype(f32)

    @pl.when(block > 0)
    def _():
        ext[0:HALO] = ext[BLOCK : BLOCK + HALO]

    now = raw.astype(f32)
    ext[HALO : HALO + BLOCK] = now
    summed = bias + weights[CONV - 1 : CONV] * now
    for back in range(1, CONV):
        kept = jnp.where(age >= back, 1.0, 0.0)
        older = ext[HALO - back : HALO - back + BLOCK]
        summed = summed + weights[CONV - 1 - back : CONV - back] * (older * kept)
    return silu(summed).astype(bf16)


def wide_row(ref, at):
    return jnp.concatenate([ref[pl.ds(at, 1), :], ref[pl.ds(at + 1, 1), :]], axis=1)


def ends_kernel(
    place, x_in, b_in, halo, dt_in, x_w, x_b, b_w, b_b, dt_bias, a_log, doc_len,
    x_out, b_out, states_out, sent, ext_x, ext_b, state, total, x_raw, b_raw, arrived,
):
    block = pl.program_id(0)
    blocks = pl.num_programs(0)
    group, first = place[0], place[1]
    columns = pl.ds(pl.multiple_of(group * STATE, STATE), STATE)
    copies = (
        pltpu.make_async_copy(x_in, x_raw, arrived.at[0]),
        pltpu.make_async_copy(b_in.at[:, columns], b_raw, arrived.at[1]),
    )

    @pl.when(block == 0)
    def _():
        for copy in copies:
            copy.start()
        state[...] = jnp.zeros_like(state)
        total[...] = jnp.zeros_like(total)
        for copy in copies:
            copy.wait()

    here = pl.ds(pl.multiple_of(block * BLOCK, BLOCK), BLOCK)
    start, places = doc_starts(doc_len[...], first + block * BLOCK)
    age = places - start
    width = x_in.shape[1]
    x = conv_silu(block, ext_x, halo[:, :width], x_raw[here], x_w[...], wide_row(x_b, 0), age)
    b = conv_silu(
        block, ext_b, halo[:, width : width + STATE], b_raw[here], b_w[...],
        wide_row(b_b, 2 * group), age,
    )
    x_out[...] = x
    b_out[...] = b
    step, decay = steps(dt_in[...], dt_bias, a_log)
    upto = (iota((BLOCK, BLOCK), 0) <= iota((BLOCK, BLOCK), 1)).astype(f32)
    running = dot(decay, upto, exact_mode)
    last = running[:, BLOCK - 1 : BLOCK]
    last_start = start[BLOCK - 1 : BLOCK]
    ahead = (iota((1, BLOCK), 1) + first + block * BLOCK).astype(f32)
    tail = jnp.where(ahead >= last_start, jnp.exp(last - running), 0.0) * step
    block_start = (first + block * BLOCK).astype(f32)
    carry = jnp.where(last_start < block_start, jnp.exp(last), 0.0)
    heads = dt_in.shape[0]
    old = state[...]
    states_out[0] = old.astype(bf16)
    across = jnp.transpose(x.astype(f32))
    scaled, kept = [], []
    for head in range(heads):
        rows = slice(head * HEAD_DIM, (head + 1) * HEAD_DIM)
        scaled.append(across[rows] * tail[head : head + 1])
        kept.append(old[rows] * carry[head : head + 1])
    high, low = split_pair(jnp.concatenate(scaled, axis=0))
    new = jnp.concatenate(kept, axis=0) + dot(high, b) + dot(low, b)
    state[...] = new
    total[...] = total[...] + last

    @pl.when(block == blocks - 1)
    def _():
        count = sent.shape[0]
        shard_start = first.astype(f32)
        through = jnp.where(last_start < shard_start, jnp.exp(total[...]), 0.0)
        top = through.astype(bf16).astype(f32)
        middle = (through - top).astype(bf16).astype(f32)
        rest = through - top - middle
        lane = iota((8, 128), 1)
        for piece in range(count):
            rows = 2 * HALO * piece
            head = piece * heads // count
            sent[piece, :, :STATE] = new[rows : rows + HALO].astype(bf16)
            sent[piece, :, STATE : 2 * STATE] = new[rows + HALO : rows + 2 * HALO].astype(bf16)
            one = slice(head, head + 1)
            extra = jnp.where(lane == 0, top[one], jnp.where(lane == 1, middle[one], rest[one]))
            sent[piece, :, 2 * STATE :] = extra.astype(bf16)


def spread(columns):
    lane = iota((BLOCK, 128), 1)
    return jnp.concatenate(
        [
            jnp.where(lane < HEAD_DIM, columns[:, at : at + 1], columns[:, at + 1 : at + 2])
            for at in (0, 2)
        ],
        axis=1,
    )


def inside_kernel(
    place, x_ref, b_ref, c_in, z_in, halo, dt_in, c_w, c_b, states, dt_bias, a_log, skip, doc_len,
    c_out, base_out, gain_out, ext_c, total, c_raw, arrived,
):
    block = pl.program_id(0)
    group, first = place[0], place[1]

    @pl.when(block == 0)
    def _():
        columns = pl.ds(pl.multiple_of((GROUPS + group) * STATE, STATE), STATE)
        copy = pltpu.make_async_copy(c_in.at[:, columns], c_raw, arrived)
        copy.start()
        copy.wait()

    here = pl.ds(pl.multiple_of(block * BLOCK, BLOCK), BLOCK)
    start, places = doc_starts(doc_len[...], first + block * BLOCK)
    c = conv_silu(
        block, ext_c, halo[:, 2 * STATE : 3 * STATE], c_raw[here], c_w[...],
        wide_row(c_b, 2 * (GROUPS + group)), places - start,
    )
    c_out[...] = c
    step, decay = steps(dt_in[...], dt_bias, a_log)
    older = iota((BLOCK, BLOCK), 1) <= iota((BLOCK, BLOCK), 0)
    tri = older.astype(f32)
    down = dot_rows(tri, decay, exact_mode)
    running = dot_rows(decay, tri, exact_mode)
    ahead = (iota((1, BLOCK), 1) + first + block * BLOCK).astype(f32)
    same = older & (ahead >= start)
    inner = dot_rows(c, b_ref[...])
    x = x_ref[...]
    x_wide = x.astype(f32)
    column = iota((BLOCK, x.shape[1]), 1)
    heads = dt_in.shape[0]
    y = jnp.zeros((BLOCK, x.shape[1]), f32)
    gains = jnp.zeros((1, x.shape[1]), f32)
    for head in range(heads):
        gap = jnp.minimum(down[:, head : head + 1] - running[head : head + 1], 0.0)
        mixing = jnp.where(same, jnp.exp(gap), 0.0) * step[head : head + 1] * inner
        own = (column >= head * HEAD_DIM) & (column < (head + 1) * HEAD_DIM)
        y = y + dot(mixing.astype(bf16), jnp.where(own, x_wide, 0.0).astype(bf16))
        gains = jnp.where(own[0:1], skip[head], gains)

    @pl.when(block == 0)
    def _():
        total[...] = jnp.zeros_like(total)

    block_start = (first + block * BLOCK).astype(f32)
    local = jnp.where(start < block_start, jnp.exp(down), 0.0)
    far = jnp.where(start < first.astype(f32), jnp.exp(down + total[...]), 0.0)
    total[...] = total[...] + down[BLOCK - 1 : BLOCK]
    y = y + dot_rows(c, states[0]) * spread(local) + gains * x_wide
    gate = silu(z_in[...].astype(f32))
    base_out[...] = y * gate
    gain_out[...] = spread(far) * gate


def scan_kernel(got, back):
    now = jnp.zeros((HALO, 2 * STATE), f32)
    for shard in range(got.shape[0]):
        back[shard] = now.astype(bf16)
        message = got[shard].astype(f32)
        at = 2 * STATE
        factor = message[0:1, at : at + 1] + message[0:1, at + 1 : at + 2]
        factor = factor + message[0:1, at + 2 : at + 3]
        now = factor * now + message[:, :at]


def join_kernel(mine, c_ref, base, gain, gated_out, copies):
    rows = []
    for piece in range(mine.shape[0]):
        part = mine[piece].astype(f32)
        rows += [part[:, :STATE], part[:, STATE:]]
    entering = jnp.concatenate(rows, axis=0).astype(bf16)
    ones = jnp.ones((8, base.shape[1]), bf16)
    squares = []
    for block in range(base.shape[0] // BLOCK):
        here = slice(block * BLOCK, (block + 1) * BLOCK)
        gated = base[here] + gain[here] * dot_rows(c_ref[here], entering)
        gated_out[here] = gated
        high, low = split_pair(gated * gated)
        sums = dot_rows(ones, high) + dot_rows(ones, low)
        squares += [sums[0:1, :128], sums[0:1, 128:]]
    packed = jnp.concatenate(squares, axis=0).astype(bf16)
    copies[...] = jnp.broadcast_to(packed[None], copies.shape)


def finish_kernel(channels, everything, gated, norm, out, scale):
    block = pl.program_id(0)

    @pl.when(block == 0)
    def _():
        total = jnp.sum(everything[...].astype(f32), axis=0)
        scale[...] = lax.rsqrt(total / channels + norm_floor)

    same = iota((128, 128), 0) == iota((128, 128), 1)
    columns = []
    for half in range(2):
        row = scale[pl.ds(2 * block + half, 1), :]
        columns.append(jnp.sum(jnp.where(same, row, 0.0), axis=1, keepdims=True))
    column = jnp.concatenate(columns, axis=0)
    out[...] = (gated[...] * column * wide_row(norm, 0)).astype(bf16)


def shards(
    x_in, bc_in, z_in, dt_in, conv_x_w, conv_x_b, conv_bc_w, conv_bc_b, dt_bias, a_log,
    skip_gain, norm_w, doc_len,
):
    rows, width = x_in.shape
    heads = dt_in.shape[0]
    heads_total = heads * lax.axis_size("head")
    per_group = heads_total // GROUPS
    group = lax.axis_index("head") * heads // per_group
    place = jnp.stack([group, lax.axis_index("context") * rows]).astype(jnp.int32)
    shard_count = lax.axis_size("context")
    head_count = lax.axis_size("head")
    blocks = rows // BLOCK

    bc_last = bc_in[rows - HALO :]
    last = jnp.concatenate(
        [
            x_in[rows - HALO :],
            lax.dynamic_slice_in_dim(bc_last, group * STATE, STATE, 1),
            lax.dynamic_slice_in_dim(bc_last, (GROUPS + group) * STATE, STATE, 1),
        ],
        axis=1,
    )
    pairs = [(i, i + 1) for i in range(shard_count - 1)]
    halo = lax.ppermute(last, "context", pairs)
    x_b = conv_x_b.reshape(-1, 128)
    bc_b = conv_bc_b.reshape(-1, 128)
    norm = norm_w.reshape(-1, 128)
    docs = doc_len.reshape(1, -1)

    def whole(*shape):
        return pl.BlockSpec(shape, lambda i, *_: (0,) * len(shape))

    tokens = pl.BlockSpec((BLOCK, width), lambda i, *_: (i, 0))
    in_place = pl.BlockSpec(memory_space=pltpu.HBM)
    b_taps = pl.BlockSpec((CONV, STATE), lambda i, s: (0, s[0]))
    c_taps = pl.BlockSpec((CONV, STATE), lambda i, s: (0, s[0] + GROUPS))
    dt_cols = pl.BlockSpec((heads, BLOCK), lambda i, *_: (0, i))
    scalars = pl.BlockSpec(memory_space=pltpu.SMEM)
    block_states = pl.BlockSpec((1, width, STATE), lambda i, *_: (i, 0, 0))

    def call(kernel, prefetch, in_specs, out_specs, out_shape, scratch, grant=GRANT):
        return pl.pallas_call(
            kernel,
            grid_spec=pltpu.PrefetchScalarGridSpec(
                num_scalar_prefetch=prefetch,
                grid=(blocks,),
                in_specs=in_specs,
                out_specs=out_specs,
                scratch_shapes=scratch,
            ),
            out_shape=out_shape,
            compiler_params=pltpu.CompilerParams(vmem_limit_bytes=grant),
            cost_estimate=pl.CostEstimate(
                flops=500_000_000, bytes_accessed=4_000_000, transcendentals=1_000_000
            ),
        )

    struct = jax.ShapeDtypeStruct
    message = 2 * STATE + 128
    x, b, states, sent = call(
        ends_kernel,
        1,
        [
            in_place, in_place, whole(HALO, width + 2 * STATE), dt_cols, whole(CONV, width),
            whole(*x_b.shape), b_taps, whole(*bc_b.shape), scalars, scalars, whole(*docs.shape),
        ],
        [tokens, tokens, block_states, whole(shard_count, HALO, message)],
        [
            struct((rows, width), bf16),
            struct((rows, STATE), bf16),
            struct((blocks, width, STATE), bf16),
            struct((shard_count, HALO, message), bf16),
        ],
        [
            pltpu.VMEM((BLOCK + HALO, width), f32),
            pltpu.VMEM((BLOCK + HALO, STATE), f32),
            pltpu.VMEM((width, STATE), f32),
            pltpu.VMEM((8, 1), f32),
            pltpu.VMEM((rows, width), bf16),
            pltpu.VMEM((rows, STATE), bf16),
            pltpu.SemaphoreType.DMA((2,)),
        ],
        WIDE_GRANT,
    )(place, x_in, bc_in, halo, dt_in, conv_x_w, x_b, conv_bc_w, bc_b, dt_bias, a_log, docs)
    got = lax.all_to_all(sent, "context", split_axis=0, concat_axis=0, tiled=True)
    c, base, gain = call(
        inside_kernel,
        1,
        [
            tokens, tokens, in_place, tokens, whole(HALO, width + 2 * STATE), dt_cols, c_taps,
            whole(*bc_b.shape), block_states, scalars, scalars, scalars, whole(*docs.shape),
        ],
        [tokens, tokens, tokens],
        [
            struct((rows, STATE), bf16),
            struct((rows, width), f32),
            struct((rows, width), f32),
        ],
        [
            pltpu.VMEM((BLOCK + HALO, STATE), f32),
            pltpu.VMEM((1, 8), f32),
            pltpu.VMEM((rows, STATE), bf16),
            pltpu.SemaphoreType.DMA,
        ],
        WIDE_GRANT,
    )(
        place, x, b, bc_in, z_in, halo, dt_in, conv_bc_w, bc_b, states, dt_bias, a_log,
        skip_gain, docs,
    )
    back = pl.pallas_call(
        scan_kernel,
        out_shape=struct((shard_count, HALO, 2 * STATE), bf16),
        compiler_params=pltpu.CompilerParams(vmem_limit_bytes=GRANT),
    )(got)
    mine = lax.all_to_all(back, "context", split_axis=0, concat_axis=0, tiled=True)
    gated, copies = pl.pallas_call(
        join_kernel,
        out_shape=[
            struct((rows, width), f32),
            struct((head_count, rows // 128, 128), bf16),
        ],
        compiler_params=pltpu.CompilerParams(vmem_limit_bytes=GRANT),
    )(mine, c, base, gain)
    everything = lax.all_to_all(copies, "head", split_axis=0, concat_axis=0, tiled=True)
    return call(
        functools.partial(finish_kernel, float(heads_total * HEAD_DIM)),
        0,
        [whole(head_count, rows // 128, 128), tokens, whole(*norm.shape)],
        tokens,
        struct((rows, width), bf16),
        [pltpu.VMEM((rows // 128, 128), f32)],
    )(everything, gated, norm)


def solution(mesh):
    return jax.shard_map(
        shards,
        mesh=mesh,
        in_specs=(
            P("context", "head"),
            P("context", None),
            P("context", "head"),
            P("head", "context"),
            P(None, "head"),
            P("head"),
            P(),
            P(),
            P("head"),
            P("head"),
            P("head"),
            P("head"),
            P(),
        ),
        out_specs=P("context", "head"),
        check_vma=False,
    )
```
